32 devices in a mesh: dp: 8 (over z, x), row: 2 (over core), col: 2 (over y).
Axes of the slice: x: 2, y: 2, z: 4, core: 2. Of those that a mesh axis runs over, the one named last changes fastest.
Arguments:
- hidden_in: bfloat16 [4096, 640], P(('dp', 'row'), 'col'), may hold values from -6 to 6
- cotangent: bfloat16 [4096, 640], P(('dp', 'row'), 'col'), may hold values from -6 to 6
- positions: int32 [16, 256], P(('dp', 'col')), may hold values from 0 to 255, as said below
- q_weight: bfloat16 [640, 1024], P('col', 'row'), may hold values from -0.25 to 0.25
- kv_weight: bfloat16 [640, 512], P('col', 'row'), may hold values from -0.25 to 0.25
- o_weight: bfloat16 [1024, 640], P('row', 'col'), may hold values from -0.1875 to 0.1875
- gate_weight: bfloat16 [640, 2048], P('col', 'row'), may hold values from -0.25 to 0.25
- up_weight: bfloat16 [640, 2048], P('col', 'row'), may hold values from -0.25 to 0.25
- down_weight: bfloat16 [2048, 640], P('row', 'col'), may hold values from -0.125 to 0.125
- norm_in: float32 [640], P('col'), may hold values from 0.25 to 1.75
- norm_attn: float32 [640], P('col'), may hold values from 0.25 to 1.75
- norm_ffn_in: float32 [640], P('col'), may hold values from 0.25 to 1.75
- norm_ffn_out: float32 [640], P('col'), may hold values from 0.25 to 1.75
- q_gain: float32 [256], replicated, may hold values from 0.25 to 1.75
- k_gain: float32 [256], replicated, may hold values from 0.25 to 1.75
Outputs:
- output_hidden: bfloat16 [4096, 640], P(('dp', 'row'), 'col')
- input_grad: float32 [4096, 640], P(('dp', 'row'), 'col')
- q_weight_grad: float32 [640, 1024], P('col', 'row')
- kv_weight_grad: float32 [640, 512], P('col', 'row')
- o_weight_grad: float32 [1024, 640], P('row', 'col')
- gate_weight_grad: float32 [640, 2048], P('col', 'row')
- up_weight_grad: float32 [640, 2048], P('col', 'row')
- down_weight_grad: float32 [2048, 640], P('row', 'col')
- norm_in_grad: float32 [640], P('col')
- norm_attn_grad: float32 [640], P('col')
- norm_ffn_in_grad: float32 [640], P('col')
- norm_ffn_out_grad: float32 [640], P('col')
- q_gain_grad: float32 [256], replicated
- k_gain_grad: float32 [256], replicated
The draws below stay inside these ranges and needn't reach their ends.
Inputs may be any that keep to these rules, and one draw needn't show every extreme that they name: Each row is one sequence; positions count 0, 1, 2, ... from the start of each document, the first token of a row starts a document, a row holds one to three documents, and some row is a single document.
All inputs are finite; a program needn't handle non-finite values.
Results may differ from the reference program's by a relative error of at most 0.014.
Values may be sent and summed in bfloat16 or wider, within the bound.
A program may use at most 64 MiB of HBM per device.

```python
import math
import jax
import jax.numpy as jnp
from jax import lax

D = 640
HEADS = 4
HEAD_DIM = 256
FF = 2048
WINDOW = 192
SEQ_LEN = 256
SEQS = 16
TOKENS = 4096


def draw_positions(key, part):
    cut_points = jax.random.randint(key, (SEQS, 2), 1, 2 * SEQ_LEN)
    seq_index = jnp.arange(SEQS, dtype=jnp.int32)
    cut_points = jnp.where(seq_index[:, None] == 0, 2 * SEQ_LEN, cut_points).astype(jnp.int32)
    token_index = jnp.arange(SEQ_LEN, dtype=jnp.int32)
    reached = cut_points[:, :, None] <= token_index[None, None, :]
    doc_start = jnp.max(jnp.where(reached, cut_points[:, :, None], 0), axis=1)
    return (token_index[None, :] - doc_start).astype(jnp.int32)


def steps_of(key, shape, pieces, low, largest):
    def one(axis_at, parts):
        heights = jax.random.uniform(jax.random.fold_in(jax.random.fold_in(key, 6), axis_at), (parts,), jnp.float32, low / len(pieces), largest / len(pieces))
        return jnp.repeat(jnp.exp(heights), shape[axis_at] // parts).reshape((-1,) + (1,) * (len(shape) - axis_at - 1))

    loudness = one(*pieces[0])
    for cut in pieces[1:]:
        loudness = loudness * one(*cut)
    return loudness


def noise(own_key, dims, scale, reach, shards=(), kind=jnp.bfloat16):
    result = scale * jax.random.normal(own_key, dims, jnp.float32)
    if shards:
        result = result * steps_of(own_key, dims, shards, -0.22, 0.18)
    return jnp.clip(result, -reach, reach).astype(kind)


def setup_inputs(seed: int = 0) -> dict:
    arg_keys = jax.random.split(jax.random.key(seed), 16)
    return {
        "hidden_in": noise(arg_keys[0], (TOKENS, D), 1.0, 6.0, ((0, 16), (1, 2))),
        "cotangent": noise(arg_keys[1], (TOKENS, D), 1.0, 6.0, ((0, 16), (1, 2))),
        "positions": draw_positions(jax.random.fold_in(arg_keys[15], 71), 0),
        "q_weight": noise(arg_keys[3], (D, HEADS * HEAD_DIM), D ** -0.5, 0.25, ((0, 2), (1, 2))),
        "kv_weight": noise(arg_keys[4], (D, 2 * HEAD_DIM), D ** -0.5, 0.25, ((0, 2), (1, 2))),
        "o_weight": noise(arg_keys[5], (HEADS * HEAD_DIM, D), (HEADS * HEAD_DIM) ** -0.5, 0.1875, ((0, 2), (1, 2))),
        "gate_weight": noise(arg_keys[6], (D, FF), D ** -0.5, 0.25, ((0, 2), (1, 2))),
        "up_weight": noise(arg_keys[7], (D, FF), D ** -0.5, 0.25, ((0, 2), (1, 2))),
        "down_weight": noise(arg_keys[8], (FF, D), FF ** -0.5, 0.125, ((0, 2), (1, 2))),
        "norm_in": jnp.clip(1.0 + 0.15 * jax.random.normal(arg_keys[9], (D,), jnp.float32), 0.25, 1.75),
        "norm_attn": jnp.clip(1.0 + 0.15 * jax.random.normal(arg_keys[10], (D,), jnp.float32), 0.25, 1.75),
        "norm_ffn_in": jnp.clip(1.0 + 0.15 * jax.random.normal(arg_keys[11], (D,), jnp.float32), 0.25, 1.75),
        "norm_ffn_out": jnp.clip(1.0 + 0.15 * jax.random.normal(arg_keys[12], (D,), jnp.float32), 0.25, 1.75),
        "q_gain": jnp.clip(1.0 + 0.15 * jax.random.normal(arg_keys[13], (HEAD_DIM,), jnp.float32), 0.25, 1.75),
        "k_gain": jnp.clip(1.0 + 0.15 * jax.random.normal(arg_keys[14], (HEAD_DIM,), jnp.float32), 0.25, 1.75),
    }


EPSILON = 1e-06
MASKED = -1e+30
ROPE_BASE = 10000.0

def inverse_rms(values):
    return lax.rsqrt(lax.optimization_barrier(jnp.mean(values * values, axis=-1, keepdims=True)) + EPSILON)

def norm_back(upstream, unit_part, inverse):
    return inverse * (upstream - unit_part * lax.optimization_barrier(jnp.mean(upstream * unit_part, axis=-1, keepdims=True)))

def rope_tables(token_positions):
    half_dim = HEAD_DIM // 2
    frequency = jnp.exp(jnp.arange(half_dim, dtype=jnp.float32) * (-2.0 * math.log(ROPE_BASE) / HEAD_DIM))
    angles = token_positions.astype(jnp.float32)[:, None] * frequency[None, :]
    return (jnp.cos(angles), jnp.sin(angles))

def rotate(values, cosine, sine_table):
    half_dim = values.shape[-1] // 2
    first_half = values[..., :half_dim]
    second_half = values[..., half_dim:]
    return jnp.concatenate([first_half * cosine - second_half * sine_table, second_half * cosine + first_half * sine_table], axis=-1)

def rotate_back(upstream, cosine, sine_table):
    half_dim = upstream.shape[-1] // 2
    first_half = upstream[..., :half_dim]
    second_half = upstream[..., half_dim:]
    return jnp.concatenate([first_half * cosine + second_half * sine_table, second_half * cosine - first_half * sine_table], axis=-1)

def allowed_pairs(token_positions):
    token_index = jnp.arange(token_positions.shape[0], dtype=jnp.int32)
    distance = token_index[:, None] - token_index[None, :]
    same_doc = token_positions[:, None] - token_positions[None, :] == distance
    return (distance >= 0) & (distance < WINDOW) & same_doc

def masked_scores(queries, key_rows, token_positions):
    scores = jnp.einsum('qhd,kd->hqk', queries.astype(jnp.float32), key_rows.astype(jnp.float32)) * HEAD_DIM ** (-0.5)
    return jnp.where(allowed_pairs(token_positions)[None], scores, MASKED)

def attend(queries, key_rows, value_rows, token_positions):
    scores = masked_scores(queries, key_rows, token_positions)
    row_peak = lax.optimization_barrier(jnp.max(scores, axis=-1, keepdims=True))
    log_total = row_peak + jnp.log(lax.optimization_barrier(jnp.sum(jnp.exp(scores - row_peak), axis=-1, keepdims=True)))
    probs_low = jnp.exp(scores - log_total).astype(jnp.bfloat16)
    mixed = jnp.einsum('hqk,kd->qhd', probs_low.astype(jnp.float32), value_rows.astype(jnp.float32)).astype(jnp.bfloat16)
    return (mixed, log_total)

def attend_back(queries, key_rows, value_rows, token_positions, log_total, upstream):
    scores = masked_scores(queries, key_rows, token_positions)
    probs = jnp.exp(scores - log_total)
    probs_low = probs.astype(jnp.bfloat16)
    upstream_f = upstream.astype(jnp.float32)
    d_probs = jnp.einsum('qhd,kd->hqk', upstream_f, value_rows.astype(jnp.float32))
    delta_rows = lax.optimization_barrier(jnp.sum(probs * d_probs, axis=-1, keepdims=True))
    d_scores = (probs * (d_probs - delta_rows) * HEAD_DIM ** (-0.5)).astype(jnp.bfloat16).astype(jnp.float32)
    d_queries = jnp.einsum('hqk,kd->qhd', d_scores, key_rows.astype(jnp.float32))
    d_keys = jnp.einsum('hqk,qhd->kd', d_scores, queries.astype(jnp.float32))
    d_values = jnp.einsum('hqk,qhd->kd', probs_low.astype(jnp.float32), upstream_f)
    return (d_queries, d_keys, d_values)

def gelu_tanh(values):
    return jax.nn.gelu(values, approximate=True)

def gelu_back(gate_pre, upstream):
    return jax.vjp(gelu_tanh, gate_pre)[1](upstream)[0]

def matmul(left_side, right_side):
    return jnp.dot(left_side, right_side, preferred_element_type=jnp.float32)

def layer_group(weights, hidden_in, cotangent, token_positions):
    q_weight, kv_weight, o_weight, gate_weight, up_weight, down_weight, norm_in, norm_attn, norm_ffn_in, norm_ffn_out, q_gain, k_gain = weights
    token_count = hidden_in.shape[0]
    seq_count = token_positions.shape[0]
    seq_length = token_positions.shape[1]
    x_float = hidden_in.astype(jnp.float32)
    scale_in = inverse_rms(x_float)
    unit_in = x_float * scale_in
    normed = (unit_in * norm_in).astype(jnp.bfloat16)
    q_raw = matmul(normed, q_weight).reshape(token_count, HEADS, HEAD_DIM)
    kv_raw = matmul(normed, kv_weight)
    k_raw = kv_raw[:, :HEAD_DIM]
    scale_q = inverse_rms(q_raw)
    unit_q = q_raw * scale_q
    scale_k = inverse_rms(k_raw)
    unit_k = k_raw * scale_k
    cosine, sine_table = rope_tables(token_positions.reshape(-1))
    queries = rotate(unit_q * q_gain, cosine[:, None, :], sine_table[:, None, :]).astype(jnp.bfloat16)
    key_rows = rotate(unit_k * k_gain, cosine, sine_table).astype(jnp.bfloat16)
    value_rows = kv_raw[:, HEAD_DIM:].astype(jnp.bfloat16)
    q_seq = queries.reshape(seq_count, seq_length, HEADS, HEAD_DIM)
    k_seq = key_rows.reshape(seq_count, seq_length, HEAD_DIM)
    v_seq = value_rows.reshape(seq_count, seq_length, HEAD_DIM)
    mixed, log_total = jax.vmap(attend)(q_seq, k_seq, v_seq, token_positions)
    attn = mixed.reshape(token_count, HEADS * HEAD_DIM)
    out_attn = matmul(attn, o_weight)
    scale_attn = inverse_rms(out_attn)
    unit_attn = out_attn * scale_attn
    middle = x_float + unit_attn * norm_attn
    scale_mid = inverse_rms(middle)
    unit_mid = middle * scale_mid
    ffn_in = (unit_mid * norm_ffn_in).astype(jnp.bfloat16)
    gate_pre = matmul(ffn_in, gate_weight)
    up_value = matmul(ffn_in, up_weight)
    active = gelu_tanh(gate_pre)
    hidden = (active * up_value).astype(jnp.bfloat16)
    ffn_out = matmul(hidden, down_weight)
    scale_out = inverse_rms(ffn_out)
    unit_out = ffn_out * scale_out
    output_hidden = (middle + unit_out * norm_ffn_out).astype(jnp.bfloat16)
    dy_float = cotangent.astype(jnp.float32)
    norm_ffn_out_grad = lax.optimization_barrier(jnp.sum(dy_float * unit_out, axis=0))
    d_ffn_out = norm_back(dy_float * norm_ffn_out, unit_out, scale_out).astype(jnp.bfloat16)
    down_weight_grad = matmul(hidden.T, d_ffn_out)
    d_hidden = matmul(d_ffn_out, down_weight.T)
    d_gate = gelu_back(gate_pre, d_hidden * up_value).astype(jnp.bfloat16)
    d_up = (d_hidden * active).astype(jnp.bfloat16)
    gate_weight_grad = matmul(ffn_in.T, d_gate)
    up_weight_grad = matmul(ffn_in.T, d_up)
    d_ffn_in = matmul(d_gate, gate_weight.T) + matmul(d_up, up_weight.T)
    norm_ffn_in_grad = lax.optimization_barrier(jnp.sum(d_ffn_in * unit_mid, axis=0))
    d_middle = dy_float + norm_back(d_ffn_in * norm_ffn_in, unit_mid, scale_mid)
    norm_attn_grad = lax.optimization_barrier(jnp.sum(d_middle * unit_attn, axis=0))
    d_out_attn = norm_back(d_middle * norm_attn, unit_attn, scale_attn).astype(jnp.bfloat16)
    o_weight_grad = matmul(attn.T, d_out_attn)
    d_attn = matmul(d_out_attn, o_weight.T).astype(jnp.bfloat16)
    d_attn_seq = d_attn.reshape(seq_count, seq_length, HEADS, HEAD_DIM)
    d_queries, d_keys, d_values = jax.vmap(attend_back)(q_seq, k_seq, v_seq, token_positions, log_total, d_attn_seq)
    d_queries = d_queries.reshape(token_count, HEADS, HEAD_DIM)
    d_keys = d_keys.reshape(token_count, HEAD_DIM)
    d_values = d_values.reshape(token_count, HEAD_DIM)
    q_back = rotate_back(d_queries, cosine[:, None, :], sine_table[:, None, :])
    k_back = rotate_back(d_keys, cosine, sine_table)
    q_gain_grad = lax.optimization_barrier(jnp.sum(q_back * unit_q, axis=(0, 1)))
    k_gain_grad = lax.optimization_barrier(jnp.sum(k_back * unit_k, axis=0))
    d_q = norm_back(q_back * q_gain, unit_q, scale_q).reshape(token_count, HEADS * HEAD_DIM).astype(jnp.bfloat16)
    d_k = norm_back(k_back * k_gain, unit_k, scale_k)
    d_kv = jnp.concatenate([d_k, d_values], axis=1).astype(jnp.bfloat16)
    q_weight_grad = matmul(normed.T, d_q)
    kv_weight_grad = matmul(normed.T, d_kv)
    d_normed = matmul(d_q, q_weight.T) + matmul(d_kv, kv_weight.T)
    norm_in_grad = lax.optimization_barrier(jnp.sum(d_normed * unit_in, axis=0))
    input_grad = d_middle + norm_back(d_normed * norm_in, unit_in, scale_in)
    grads = (q_weight_grad, kv_weight_grad, o_weight_grad, gate_weight_grad, up_weight_grad, down_weight_grad, norm_in_grad, norm_attn_grad, norm_ffn_in_grad, norm_ffn_out_grad, q_gain_grad, k_gain_grad)
    return (output_hidden, input_grad, grads)

def reference(hidden_in, cotangent, positions, q_weight, kv_weight, o_weight, gate_weight, up_weight, down_weight, norm_in, norm_attn, norm_ffn_in, norm_ffn_out, q_gain, k_gain):
    weights = (q_weight, kv_weight, o_weight, gate_weight, up_weight, down_weight, norm_in, norm_attn, norm_ffn_in, norm_ffn_out, q_gain, k_gain)
    group_count = SEQS // 2
    hidden_groups = hidden_in.reshape(group_count, 2 * SEQ_LEN, D)
    cotangent_groups = cotangent.reshape(group_count, 2 * SEQ_LEN, D)
    position_groups = positions.reshape(group_count, 2, SEQ_LEN)
    initial = tuple((jnp.zeros(weight.shape, jnp.float32) for weight in weights))

    def step(carry, item):
        output_hidden, input_grad, grads = layer_group(weights, item[0], item[1], item[2])
        summed = tuple((before + after for before, after in zip(carry, grads)))
        return (summed, (output_hidden, input_grad))
    final, stacked = lax.scan(step, initial, (hidden_groups, cotangent_groups, position_groups))
    output_hidden = stacked[0].reshape(TOKENS, D)
    input_grad = stacked[1].reshape(TOKENS, D)
    return (output_hidden, input_grad, final[0], final[1], final[2], final[3], final[4], final[5], final[6], final[7], final[8], final[9], final[10], final[11])
```

```python
import math

import jax
import jax.numpy as jnp
from jax import lax
from jax.sharding import PartitionSpec as P

HEAD_DIM = 256
WINDOW = 192


EPSILON = 1e-06
MASKED = -1e30
ROPE_BASE = 10000.0


def swapped(array, axis, apart):
    return lax.ppermute(array, axis, [(i, i ^ 1 << apart) for i in range(lax.axis_size(axis))])


def inverse_rms(values):
    return lax.rsqrt(jnp.mean(values * values, axis=-1, keepdims=True) + EPSILON)


def norm_back(upstream, unit_part, inverse):
    return inverse * (upstream - unit_part * jnp.mean(upstream * unit_part, axis=-1, keepdims=True))


def rope_tables(token_positions):
    half_dim = HEAD_DIM // 2
    frequency = jnp.exp(
        jnp.arange(half_dim, dtype=jnp.float32) * (-2.0 * math.log(ROPE_BASE) / HEAD_DIM)
    )
    angles = token_positions.astype(jnp.float32)[:, None] * frequency[None, :]
    return (jnp.cos(angles), jnp.sin(angles))


def rotate(values, cosine, sine_table):
    half_dim = values.shape[-1] // 2
    first_half = values[..., :half_dim]
    second_half = values[..., half_dim:]
    return jnp.concatenate(
        [
            first_half * cosine - second_half * sine_table,
            second_half * cosine + first_half * sine_table,
        ],
        axis=-1,
    )


def rotate_back(upstream, cosine, sine_table):
    half_dim = upstream.shape[-1] // 2
    first_half = upstream[..., :half_dim]
    second_half = upstream[..., half_dim:]
    return jnp.concatenate(
        [
            first_half * cosine + second_half * sine_table,
            second_half * cosine - first_half * sine_table,
        ],
        axis=-1,
    )


def allowed_pairs(token_positions):
    token_index = jnp.arange(token_positions.shape[0], dtype=jnp.int32)
    distance = token_index[:, None] - token_index[None, :]
    same_doc = token_positions[:, None] - token_positions[None, :] == distance
    return (distance >= 0) & (distance < WINDOW) & same_doc


def gelu_tanh(values):
    return jax.nn.gelu(values, approximate=True)


def gelu_back(gate_pre, upstream):
    return jax.vjp(gelu_tanh, gate_pre)[1](upstream)[0]


def product(left_side, right_side, flipped=False):
    dims = (((left_side.ndim - 1,), (1 if flipped else 0,)), ((), ()))
    return lax.dot_general(left_side, right_side, dims, preferred_element_type=jnp.float32)


def over_tokens(left_side, right_side):
    return lax.dot_general(
        left_side, right_side, (((0,), (0,)), ((), ())), preferred_element_type=jnp.float32
    )


def low(values):
    return values.astype(jnp.bfloat16)


def wide(values):
    return values.astype(jnp.float32)


def gather_rows(values):
    return jnp.concatenate([values, swapped(values, "row", 0)], axis=0)


def reduce_group(partials):
    half = partials.shape[0] // 2
    chip = partials[:half] + wide(swapped(low(partials[half:]), "row", 0))
    mine = low(chip)
    width = mine.shape[1] // 2
    theirs = swapped(mine, "col", 0)
    theirs = jnp.concatenate([theirs[:, width:], theirs[:, :width]], axis=1)
    return wide(mine) + wide(theirs)


def halves(array, axis, col_id):
    half = array.shape[axis] // 2
    first = lax.slice_in_dim(array, 0, half, axis=axis)
    second = lax.slice_in_dim(array, half, 2 * half, axis=axis)
    mine = jnp.where(col_id == 0, first, second)
    other = jnp.where(col_id == 0, second, first)
    return mine, other


def joined(mine, other, axis, col_id):
    return jnp.where(
        col_id == 0,
        jnp.concatenate([mine, other], axis=axis),
        jnp.concatenate([other, mine], axis=axis),
    )


def after(value, *earlier):
    return lax.optimization_barrier((value,) + earlier)[0]


def shards(
    hidden_in,
    cotangent,
    positions,
    q_weight,
    kv_weight,
    o_weight,
    gate_weight,
    up_weight,
    down_weight,
    norm_in,
    norm_attn,
    norm_ffn_in,
    norm_ffn_out,
    q_gain,
    k_gain,
):
    length = hidden_in.shape[0]
    block_cols = hidden_in.shape[1]
    row_id = lax.axis_index("row")
    col_id = lax.axis_index("col")
    x_other = swapped(hidden_in, "col", 0)
    q_mine, q_send = halves(q_weight, 1, col_id)
    in_send = jnp.concatenate([q_send, kv_weight], axis=1)
    in_recv = swapped(in_send, "col", 0)
    o_mine, o_send = halves(o_weight, 0, col_id)
    gate_mine, gate_send = halves(gate_weight, 1, col_id)
    up_mine, up_send = halves(up_weight, 1, col_id)
    down_mine, down_send = halves(down_weight, 0, col_id)
    ffn_send = jnp.concatenate([gate_send, up_send], axis=1)
    gains_own = jnp.stack([norm_in, norm_attn, norm_ffn_in, norm_ffn_out])
    gains = jnp.concatenate([gains_own, swapped(gains_own, "col", 0)], axis=1)
    pos_other = swapped(positions[0], "col", 0)
    o_send = after(o_send, in_recv)
    o_recv = swapped(o_send, "col", 0)
    ffn_send = after(ffn_send, o_recv)
    ffn_recv = swapped(ffn_send, "col", 0)
    down_send, dy_send = lax.optimization_barrier((down_send, cotangent, ffn_recv))[:2]
    down_recv = swapped(down_send, "col", 0)
    dy_other = swapped(dy_send, "col", 0)

    head = q_mine.shape[1]
    kv_half = kv_weight.shape[1]
    kv_rows = jnp.concatenate([kv_weight, in_recv[:, head:]], axis=0)
    kv_other = swapped(kv_rows, "row", 0)
    k_rows = jnp.where(row_id == 0, kv_rows, kv_other)
    v_rows = jnp.where(row_id == 0, kv_other, kv_rows)
    weight_in = jnp.concatenate(
        [jnp.concatenate([q_mine, in_recv[:, :head]], axis=0), k_rows, v_rows], axis=1
    )
    weight_o = jnp.concatenate([o_mine, o_recv], axis=1)
    weight_ffn = jnp.concatenate(
        [jnp.concatenate([gate_mine, up_mine], axis=1), ffn_recv], axis=0
    )
    weight_down = jnp.concatenate([down_mine, down_recv], axis=1)
    hidden_width = gate_mine.shape[1]

    same = row_id == col_id
    pos = jnp.stack(
        [jnp.where(same, positions[0], pos_other), jnp.where(same, pos_other, positions[0])]
    )
    cosine, sine_table = rope_tables(pos.reshape(-1))
    cosine = cosine.reshape(2, length, -1)
    sine_table = sine_table.reshape(2, length, -1)
    allowed = jax.vmap(allowed_pairs)(pos)

    x_float = wide(jnp.concatenate([hidden_in, x_other], axis=1))
    scale_in = inverse_rms(x_float)
    unit_in = x_float * scale_in
    normed_all = gather_rows(low(unit_in * gains[0]))
    projected = product(normed_all, weight_in).reshape(2, length, -1)
    q_raw = projected[..., :head]
    k_raw = projected[..., head : 2 * head]
    value_rows = low(projected[..., 2 * head :])
    scale_q = inverse_rms(q_raw)
    unit_q = q_raw * scale_q
    scale_k = inverse_rms(k_raw)
    unit_k = k_raw * scale_k
    queries = low(rotate(unit_q * q_gain, cosine, sine_table))
    key_rows = low(rotate(unit_k * k_gain, cosine, sine_table))
    scores = jnp.einsum(
        "bqd,bkd->bqk", queries, key_rows, preferred_element_type=jnp.float32
    ) * HEAD_DIM ** (-0.5)
    scores = jnp.where(allowed, scores, MASKED)
    row_peak = jnp.max(scores, axis=-1, keepdims=True)
    log_total = row_peak + jnp.log(jnp.sum(jnp.exp(scores - row_peak), axis=-1, keepdims=True))
    probs = jnp.exp(scores - log_total)
    probs_low = low(probs)
    attn = low(
        jnp.einsum("bqk,bkd->bqd", probs_low, value_rows, preferred_element_type=jnp.float32)
    ).reshape(2 * length, head)
    out_attn = reduce_group(product(attn, weight_o))
    scale_attn = inverse_rms(out_attn)
    unit_attn = out_attn * scale_attn
    middle = x_float + unit_attn * gains[1]
    scale_mid = inverse_rms(middle)
    unit_mid = middle * scale_mid
    ffn_all = gather_rows(low(unit_mid * gains[2]))
    gate_up = product(ffn_all, weight_ffn)
    gate_pre = gate_up[:, :hidden_width]
    up_value = gate_up[:, hidden_width:]
    active = gelu_tanh(gate_pre)
    hidden = low(active * up_value)
    ffn_out = reduce_group(product(hidden, weight_down))
    scale_out = inverse_rms(ffn_out)
    unit_out = ffn_out * scale_out
    output_hidden = low((middle + unit_out * gains[3])[:, :block_cols])

    dy_float = wide(jnp.concatenate([cotangent, dy_other], axis=1))
    d_ffn_out = low(norm_back(dy_float * gains[3], unit_out, scale_out))
    d_out_all = gather_rows(d_ffn_out)
    down_part = low(over_tokens(hidden, d_out_all))
    down_grad = joined(
        down_part[:, :block_cols], swapped(down_part[:, block_cols:], "col", 0), 0, col_id
    )
    down_grad = lax.psum(down_grad, "dp")
    d_hidden = product(d_out_all, weight_down, True)
    d_gate = gelu_back(gate_pre, d_hidden * up_value)
    d_gate_up = low(jnp.concatenate([d_gate, d_hidden * active], axis=1))
    d_ffn_in = reduce_group(product(d_gate_up, weight_ffn, True))
    ffn_part = low(over_tokens(ffn_all, d_gate_up))
    ffn_swap = swapped(ffn_part[block_cols:], "col", 0)
    gate_grad = joined(
        ffn_part[:block_cols, :hidden_width], ffn_swap[:, :hidden_width], 1, col_id
    )
    up_grad = joined(ffn_part[:block_cols, hidden_width:], ffn_swap[:, hidden_width:], 1, col_id)
    gate_grad, up_grad, _ = lax.optimization_barrier((gate_grad, up_grad, down_grad))
    gate_grad, up_grad = lax.psum((gate_grad, up_grad), "dp")
    d_middle = dy_float + norm_back(d_ffn_in * gains[2], unit_mid, scale_mid)
    d_out_attn = low(norm_back(d_middle * gains[1], unit_attn, scale_attn))
    d_attn_all = gather_rows(d_out_attn)
    o_part = low(over_tokens(attn, d_attn_all))
    o_grad = joined(o_part[:, :block_cols], swapped(o_part[:, block_cols:], "col", 0), 0, col_id)
    d_attn = low(product(d_attn_all, weight_o, True)).reshape(2, length, head)
    d_probs = jnp.einsum("bqd,bkd->bqk", d_attn, value_rows, preferred_element_type=jnp.float32)
    delta_rows = jnp.sum(probs * d_probs, axis=-1, keepdims=True)
    d_scores = low(probs * (d_probs - delta_rows) * HEAD_DIM ** (-0.5))
    d_queries = jnp.einsum("bqk,bkd->bqd", d_scores, key_rows, preferred_element_type=jnp.float32)
    d_keys = jnp.einsum("bqk,bqd->bkd", d_scores, queries, preferred_element_type=jnp.float32)
    d_values = jnp.einsum("bqk,bqd->bkd", probs_low, d_attn, preferred_element_type=jnp.float32)
    q_back = rotate_back(d_queries, cosine, sine_table)
    k_back = rotate_back(d_keys, cosine, sine_table)
    q_gain_part = jnp.sum(q_back * unit_q, axis=(0, 1))
    k_gain_part = jnp.sum(k_back * unit_k, axis=(0, 1))
    d_q = low(norm_back(q_back * q_gain, unit_q, scale_q)).reshape(2 * length, head)
    d_k = low(norm_back(k_back * k_gain, unit_k, scale_k)).reshape(2 * length, head)
    d_v = low(d_values).reshape(2 * length, head)
    d_projected = jnp.concatenate([d_q, d_k, d_v], axis=1)
    d_normed = reduce_group(product(d_projected, weight_in, True))
    kv_keep = jnp.where(row_id == 0, d_k, d_v)
    kv_send = jnp.where(row_id == 0, d_v, d_k)
    kv_send = jnp.concatenate([kv_send[length:], kv_send[:length]], axis=0)
    kv_chip = low(wide(kv_keep) + wide(swapped(kv_send, "row", 0)))
    d_kv_own = low(wide(kv_chip) + wide(swapped(kv_chip, "col", 0)))
    kv_grad = low(over_tokens(normed_all[:, :block_cols], d_kv_own))
    q_part = low(over_tokens(normed_all, d_q))
    q_grad = joined(q_part[:block_cols], swapped(q_part[block_cols:], "col", 0), 1, col_id)
    q_grad, kv_grad, o_grad = lax.optimization_barrier(
        (q_grad, kv_grad, o_grad, gate_grad, up_grad)
    )[:3]
    q_grad, kv_grad, o_grad = lax.psum((q_grad, kv_grad, o_grad), "dp")
    input_grad = d_middle + norm_back(d_normed * gains[0], unit_in, scale_in)
    gain_parts = jnp.stack(
        [
            jnp.sum(d_normed * unit_in, axis=0),
            jnp.sum(d_middle * unit_attn, axis=0),
            jnp.sum(d_ffn_in * unit_mid, axis=0),
            jnp.sum(dy_float * unit_out, axis=0),
        ]
    )[:, :block_cols]
    head_parts = jnp.stack([q_gain_part, k_gain_part])
    head_parts = head_parts + swapped(head_parts, "col", 0)
    small = jnp.concatenate([gain_parts.reshape(-1), head_parts.reshape(-1)])
    small = lax.psum(small + swapped(small, "row", 0), "dp")
    own_gains = small[: 4 * block_cols].reshape(4, block_cols)
    head_total = small[4 * block_cols :].reshape(2, head)
    return (
        output_hidden,
        input_grad[:, :block_cols],
        wide(q_grad),
        wide(kv_grad),
        wide(o_grad),
        wide(gate_grad),
        wide(up_grad),
        wide(down_grad),
        own_gains[0],
        own_gains[1],
        own_gains[2],
        own_gains[3],
        head_total[0],
        head_total[1],
    )


def solution(mesh):
    placed = (
        P(("dp", "row"), "col"),
        P(("dp", "row"), "col"),
        P(("dp", "col"), None),
        P("col", "row"),
        P("col", "row"),
        P("row", "col"),
        P("col", "row"),
        P("col", "row"),
        P("row", "col"),
        P("col"),
        P("col"),
        P("col"),
        P("col"),
        P(),
        P(),
    )
    return jax.shard_map(
        shards,
        mesh=mesh,
        in_specs=placed,
        out_specs=(
            P(("dp", "row"), "col"),
            P(("dp", "row"), "col"),
            P("col", "row"),
            P("col", "row"),
            P("row", "col"),
            P("col", "row"),
            P("col", "row"),
            P("row", "col"),
            P("col"),
            P("col"),
            P("col"),
            P("col"),
            P(),
            P(),
        ),
        check_vma=False,
    )
```

```python
import math

import jax
import jax.numpy as jnp
from jax import lax
from jax.sharding import PartitionSpec as P

HEAD_DIM = 256
WINDOW = 192


EPSILON = 1e-06
MASKED = -1e30
ROPE_BASE = 10000.0


def swapped(array, axis, apart):
    return lax.ppermute(array, axis, [(i, i ^ 1 << apart) for i in range(lax.axis_size(axis))])


def inverse_rms(values):
    return lax.rsqrt(jnp.mean(values * values, axis=-1, keepdims=True) + EPSILON)


def norm_back(upstream, unit_part, inverse):
    return inverse * (upstream - unit_part * jnp.mean(upstream * unit_part, axis=-1, keepdims=True))


def rope_tables(token_positions):
    half_dim = HEAD_DIM // 2
    frequency = jnp.exp(
        jnp.arange(half_dim, dtype=jnp.float32) * (-2.0 * math.log(ROPE_BASE) / HEAD_DIM)
    )
    angles = token_positions.astype(jnp.float32)[:, None] * frequency[None, :]
    return (jnp.cos(angles), jnp.sin(angles))


def rotate(values, cosine, sine_table):
    half_dim = values.shape[-1] // 2
    first_half = values[..., :half_dim]
    second_half = values[..., half_dim:]
    return jnp.concatenate(
        [
            first_half * cosine - second_half * sine_table,
            second_half * cosine + first_half * sine_table,
        ],
        axis=-1,
    )


def rotate_back(upstream, cosine, sine_table):
    half_dim = upstream.shape[-1] // 2
    first_half = upstream[..., :half_dim]
    second_half = upstream[..., half_dim:]
    return jnp.concatenate(
        [
            first_half * cosine + second_half * sine_table,
            second_half * cosine - first_half * sine_table,
        ],
        axis=-1,
    )


def allowed_pairs(token_positions):
    token_index = jnp.arange(token_positions.shape[0], dtype=jnp.int32)
    distance = token_index[:, None] - token_index[None, :]
    same_doc = token_positions[:, None] - token_positions[None, :] == distance
    return (distance >= 0) & (distance < WINDOW) & same_doc


def gelu_tanh(values):
    return jax.nn.gelu(values, approximate=True)


def gelu_back(gate_pre, upstream):
    return jax.vjp(gelu_tanh, gate_pre)[1](upstream)[0]


def product(left_side, right_side, flipped=False):
    dims = (((left_side.ndim - 1,), (1 if flipped else 0,)), ((), ()))
    return lax.dot_general(left_side, right_side, dims, preferred_element_type=jnp.float32)


def over_tokens(left_side, right_side):
    return lax.dot_general(
        left_side, right_side, (((0,), (0,)), ((), ())), preferred_element_type=jnp.float32
    )


def low(values):
    return values.astype(jnp.bfloat16)


def wide(values):
    return values.astype(jnp.float32)


def gather_rows(values):
    return jnp.concatenate([values, swapped(values, "row", 0)], axis=0)


def reduce_group(partials):
    half = partials.shape[0] // 2
    chip = partials[:half] + wide(swapped(low(partials[half:]), "row", 0))
    mine = low(chip)
    width = mine.shape[1] // 2
    theirs = swapped(mine, "col", 0)
    theirs = jnp.concatenate([theirs[:, width:], theirs[:, :width]], axis=1)
    return wide(mine) + wide(theirs)


def halves(array, axis, col_id):
    half = array.shape[axis] // 2
    first = lax.slice_in_dim(array, 0, half, axis=axis)
    second = lax.slice_in_dim(array, half, 2 * half, axis=axis)
    mine = jnp.where(col_id == 0, first, second)
    other = jnp.where(col_id == 0, second, first)
    return mine, other


def my_bit(bit):
    return (lax.axis_index("dp") >> bit) & 1


def dp_bits():
    return (lax.axis_size("dp") - 1).bit_length()


def scatter_sum(parts, first):
    count = dp_bits()
    kinds, rows, width = parts.shape
    cur = parts.reshape((kinds,) + (2,) * count + (rows // lax.axis_size("dp"), width))
    order = [first] + [b for b in range(count) if b != first] if count else []
    for bit in order:
        axis = count - bit
        mine = my_bit(bit)
        send = lax.dynamic_slice_in_dim(cur, 1 - mine, 1, axis)
        keep = lax.dynamic_slice_in_dim(cur, mine, 1, axis)
        cur = low(wide(keep) + wide(swapped(send, "dp", bit)))
    return cur, order


def gather_dp(cur, order):
    count = dp_bits()
    for bit in reversed(order):
        axis = count - bit
        theirs = swapped(cur, "dp", bit)
        cur = jnp.where(
            my_bit(bit) == 0,
            jnp.concatenate([cur, theirs], axis=axis),
            jnp.concatenate([theirs, cur], axis=axis),
        )
    return cur.reshape(cur.shape[0], -1, cur.shape[-1])


def total_grad(part, first, col_id, extra=None):
    width = part.shape[1]
    stacked = part.reshape(2, -1, width)
    if extra is not None:
        stacked = jnp.concatenate([stacked, extra[None]], axis=0)
    cur, order = scatter_sum(stacked, first)
    recv = swapped(cur[1:2], "col", 0)
    own = cur[:1]
    both = jnp.where(
        col_id == 0, jnp.concatenate([own, recv], axis=0), jnp.concatenate([recv, own], axis=0)
    )
    if extra is not None:
        both = jnp.concatenate([both, cur[2:]], axis=0)
    return wide(gather_dp(both, order))


def small_total(values):
    for bit in range(dp_bits()):
        values = values + swapped(values, "dp", bit)
    return values


def after(value, *earlier):
    return lax.optimization_barrier((value,) + earlier)[0]


def shards(
    hidden_in,
    cotangent,
    positions,
    q_weight,
    kv_weight,
    o_weight,
    gate_weight,
    up_weight,
    down_weight,
    norm_in,
    norm_attn,
    norm_ffn_in,
    norm_ffn_out,
    q_gain,
    k_gain,
):
    length = hidden_in.shape[0]
    block_cols = hidden_in.shape[1]
    row_id = lax.axis_index("row")
    col_id = lax.axis_index("col")
    x_other = swapped(hidden_in, "col", 0)
    q_mine, q_send = halves(q_weight, 1, col_id)
    in_send = jnp.concatenate([q_send, kv_weight], axis=1)
    in_recv = swapped(in_send, "col", 0)
    o_mine, o_send = halves(o_weight, 0, col_id)
    gate_mine, gate_send = halves(gate_weight, 1, col_id)
    up_mine, up_send = halves(up_weight, 1, col_id)
    down_mine, down_send = halves(down_weight, 0, col_id)
    ffn_send = jnp.concatenate([gate_send, up_send], axis=1)
    gains_own = jnp.stack([norm_in, norm_attn, norm_ffn_in, norm_ffn_out])
    gains = jnp.concatenate([gains_own, swapped(gains_own, "col", 0)], axis=1)
    pos_other = swapped(positions[0], "col", 0)
    o_send = after(o_send, in_recv)
    o_recv = swapped(o_send, "col", 0)
    ffn_send = after(ffn_send, o_recv)
    ffn_recv = swapped(ffn_send, "col", 0)
    down_send, dy_send = lax.optimization_barrier((down_send, cotangent, ffn_recv))[:2]
    down_recv = swapped(down_send, "col", 0)
    dy_other = swapped(dy_send, "col", 0)

    head = q_mine.shape[1]
    kv_half = kv_weight.shape[1]
    kv_rows = jnp.concatenate([kv_weight, in_recv[:, head:]], axis=0)
    kv_other = swapped(kv_rows, "row", 0)
    k_rows = jnp.where(row_id == 0, kv_rows, kv_other)
    v_rows = jnp.where(row_id == 0, kv_other, kv_rows)
    weight_in = jnp.concatenate(
        [jnp.concatenate([q_mine, in_recv[:, :head]], axis=0), k_rows, v_rows], axis=1
    )
    weight_o = jnp.concatenate([o_mine, o_recv], axis=1)
    weight_ffn = jnp.concatenate(
        [jnp.concatenate([gate_mine, up_mine], axis=1), ffn_recv], axis=0
    )
    weight_down = jnp.concatenate([down_mine, down_recv], axis=1)
    hidden_width = gate_mine.shape[1]

    same = row_id == col_id
    pos = jnp.stack(
        [jnp.where(same, positions[0], pos_other), jnp.where(same, pos_other, positions[0])]
    )
    cosine, sine_table = rope_tables(pos.reshape(-1))
    cosine = cosine.reshape(2, length, -1)
    sine_table = sine_table.reshape(2, length, -1)
    allowed = jax.vmap(allowed_pairs)(pos)

    x_float = wide(jnp.concatenate([hidden_in, x_other], axis=1))
    scale_in = inverse_rms(x_float)
    unit_in = x_float * scale_in
    normed_all = gather_rows(low(unit_in * gains[0]))
    projected = product(normed_all, weight_in).reshape(2, length, -1)
    q_raw = projected[..., :head]
    k_raw = projected[..., head : 2 * head]
    value_rows = low(projected[..., 2 * head :])
    scale_q = inverse_rms(q_raw)
    unit_q = q_raw * scale_q
    scale_k = inverse_rms(k_raw)
    unit_k = k_raw * scale_k
    queries = low(rotate(unit_q * q_gain, cosine, sine_table))
    key_rows = low(rotate(unit_k * k_gain, cosine, sine_table))
    scores = jnp.einsum(
        "bqd,bkd->bqk", queries, key_rows, preferred_element_type=jnp.float32
    ) * HEAD_DIM ** (-0.5)
    scores = jnp.where(allowed, scores, MASKED)
    row_peak = jnp.max(scores, axis=-1, keepdims=True)
    log_total = row_peak + jnp.log(jnp.sum(jnp.exp(scores - row_peak), axis=-1, keepdims=True))
    probs = jnp.exp(scores - log_total)
    probs_low = low(probs)
    attn = low(
        jnp.einsum("bqk,bkd->bqd", probs_low, value_rows, preferred_element_type=jnp.float32)
    ).reshape(2 * length, head)
    out_attn = reduce_group(product(attn, weight_o))
    scale_attn = inverse_rms(out_attn)
    unit_attn = out_attn * scale_attn
    middle = x_float + unit_attn * gains[1]
    scale_mid = inverse_rms(middle)
    unit_mid = middle * scale_mid
    ffn_all = gather_rows(low(unit_mid * gains[2]))
    gate_up = product(ffn_all, weight_ffn)
    gate_pre = gate_up[:, :hidden_width]
    up_value = gate_up[:, hidden_width:]
    active = gelu_tanh(gate_pre)
    hidden = low(active * up_value)
    ffn_out = reduce_group(product(hidden, weight_down))
    scale_out = inverse_rms(ffn_out)
    unit_out = ffn_out * scale_out
    output_hidden = low((middle + unit_out * gains[3])[:, :block_cols])

    dy_float = wide(jnp.concatenate([cotangent, dy_other], axis=1))
    d_ffn_out = low(norm_back(dy_float * gains[3], unit_out, scale_out))
    d_out_all = gather_rows(d_ffn_out)
    z_bit = 1 if dp_bits() > 1 else 0
    down_part = low(over_tokens(d_out_all, hidden))
    down_sum = total_grad(down_part, z_bit, col_id)
    down_grad = jnp.concatenate([down_sum[0], down_sum[1]], axis=1).T
    d_hidden = product(d_out_all, weight_down, True)
    d_gate = gelu_back(gate_pre, d_hidden * up_value)
    d_gate_up = low(jnp.concatenate([d_gate, d_hidden * active], axis=1))
    d_ffn_in = reduce_group(product(d_gate_up, weight_ffn, True))
    ffn_part = low(over_tokens(ffn_all, d_gate_up))
    ffn_sum = total_grad(ffn_part, 0, col_id)
    gate_grad = jnp.concatenate(
        [ffn_sum[0, :, :hidden_width], ffn_sum[1, :, :hidden_width]], axis=1
    )
    up_grad = jnp.concatenate([ffn_sum[0, :, hidden_width:], ffn_sum[1, :, hidden_width:]], axis=1)
    d_middle = dy_float + norm_back(d_ffn_in * gains[2], unit_mid, scale_mid)
    d_out_attn = low(norm_back(d_middle * gains[1], unit_attn, scale_attn))
    d_attn_all = gather_rows(d_out_attn)
    o_part = low(over_tokens(d_attn_all, attn))
    o_sum = total_grad(o_part, z_bit, col_id)
    o_grad = jnp.concatenate([o_sum[0], o_sum[1]], axis=1).T
    d_attn = low(product(d_attn_all, weight_o, True)).reshape(2, length, head)
    d_probs = jnp.einsum("bqd,bkd->bqk", d_attn, value_rows, preferred_element_type=jnp.float32)
    delta_rows = jnp.sum(probs * d_probs, axis=-1, keepdims=True)
    d_scores = low(probs * (d_probs - delta_rows) * HEAD_DIM ** (-0.5))
    d_queries = jnp.einsum("bqk,bkd->bqd", d_scores, key_rows, preferred_element_type=jnp.float32)
    d_keys = jnp.einsum("bqk,bqd->bkd", d_scores, queries, preferred_element_type=jnp.float32)
    d_values = jnp.einsum("bqk,bqd->bkd", probs_low, d_attn, preferred_element_type=jnp.float32)
    q_back = rotate_back(d_queries, cosine, sine_table)
    k_back = rotate_back(d_keys, cosine, sine_table)
    q_gain_part = jnp.sum(q_back * unit_q, axis=(0, 1))
    k_gain_part = jnp.sum(k_back * unit_k, axis=(0, 1))
    d_q = low(norm_back(q_back * q_gain, unit_q, scale_q)).reshape(2 * length, head)
    d_k = low(norm_back(k_back * k_gain, unit_k, scale_k)).reshape(2 * length, head)
    d_v = low(d_values).reshape(2 * length, head)
    d_projected = jnp.concatenate([d_q, d_k, d_v], axis=1)
    d_normed = reduce_group(product(d_projected, weight_in, True))
    kv_keep = jnp.where(row_id == 0, d_k, d_v)
    kv_send = jnp.where(row_id == 0, d_v, d_k)
    kv_send = jnp.concatenate([kv_send[length:], kv_send[:length]], axis=0)
    kv_chip = low(wide(kv_keep) + wide(swapped(kv_send, "row", 0)))
    d_kv_own = low(wide(kv_chip) + wide(swapped(kv_chip, "col", 0)))
    kv_grad = low(over_tokens(normed_all[:, :block_cols], d_kv_own))
    q_part = low(over_tokens(normed_all, d_q))
    in_sum = total_grad(q_part, 0, col_id, kv_grad)
    q_grad = jnp.concatenate([in_sum[0], in_sum[1]], axis=1)
    kv_grad = in_sum[2]
    input_grad = d_middle + norm_back(d_normed * gains[0], unit_in, scale_in)
    gain_parts = jnp.stack(
        [
            jnp.sum(d_normed * unit_in, axis=0),
            jnp.sum(d_middle * unit_attn, axis=0),
            jnp.sum(d_ffn_in * unit_mid, axis=0),
            jnp.sum(dy_float * unit_out, axis=0),
        ]
    )[:, :block_cols]
    head_parts = jnp.stack([q_gain_part, k_gain_part])
    head_parts = head_parts + swapped(head_parts, "col", 0)
    small = jnp.concatenate([gain_parts.reshape(-1), head_parts.reshape(-1)])
    small = small_total(small + swapped(small, "row", 0))
    own_gains = small[: 4 * block_cols].reshape(4, block_cols)
    head_total = small[4 * block_cols :].reshape(2, head)
    return (
        output_hidden,
        input_grad[:, :block_cols],
        q_grad,
        kv_grad,
        o_grad,
        gate_grad,
        up_grad,
        down_grad,
        own_gains[0],
        own_gains[1],
        own_gains[2],
        own_gains[3],
        head_total[0],
        head_total[1],
    )


def solution(mesh):
    placed = (
        P(("dp", "row"), "col"),
        P(("dp", "row"), "col"),
        P(("dp", "col"), None),
        P("col", "row"),
        P("col", "row"),
        P("row", "col"),
        P("col", "row"),
        P("col", "row"),
        P("row", "col"),
        P("col"),
        P("col"),
        P("col"),
        P("col"),
        P(),
        P(),
    )
    return jax.shard_map(
        shards,
        mesh=mesh,
        in_specs=placed,
        out_specs=(
            P(("dp", "row"), "col"),
            P(("dp", "row"), "col"),
            P("col", "row"),
            P("col", "row"),
            P("row", "col"),
            P("col", "row"),
            P("col", "row"),
            P("row", "col"),
            P("col"),
            P("col"),
            P("col"),
            P("col"),
            P(),
            P(),
        ),
        check_vma=False,
    )
```
